32 devices in a mesh: slab: 32 (over z, y, x, core).
Axes of the slice: x: 2, y: 2, z: 4, core: 2. Of those that a mesh axis runs over, the one named last changes fastest.
Arguments:
- load_terms: float32 [8, 8, 8, 4096], P(None, None, None, 'slab'), may hold values from -12 to 12
- geometry: float32 [3, 8, 8, 8, 4096], P(None, None, None, None, 'slab'), may hold values from 0.02 to 0.2
- mass_terms: float32 [8, 8, 8, 4096], P(None, None, None, 'slab'), may hold values from 1 to 4
- element_order: int32 [32, 128], P('slab'), may hold values from 0 to 127, each once within a row
Outputs:
- solution: float32 [8, 8, 8, 4096], P(None, None, None, 'slab')
- residual: float32 [8, 8, 8, 4096], P(None, None, None, 'slab')
The draws below stay inside these ranges and needn't reach their ends.
Inputs may be any that keep to these rules, and one draw needn't show every extreme that they name: `element_order`: each device's row lists each of its 128 cells once.
All inputs are finite; a program needn't handle non-finite values.
Results may differ from the reference program's by a relative error of at most 0.0001.
Values sent between devices are 32-bit elements; how exact they have to be, the bound alone decides.
A program may use at most 64 MiB of HBM per device.

```python
import math
import jax
import jax.numpy as jnp
import numpy as np
from jax import lax

POINTS = 8
EL_X = 1
EL_Y = 8
EL_Z = 16
SECTIONS = 2
ELEM_DEV = 128
NELEM = 4096
N_SLAB = 32


def draw_load_terms(key, part):
    noise = jax.random.normal(key, (POINTS, POINTS, POINTS, NELEM), jnp.float32)
    device_pos = (jnp.arange(NELEM) // ELEM_DEV).astype(jnp.float32)
    ramp = 1.0 + 0.8 * device_pos / max(NELEM // ELEM_DEV - 1, 1)
    return jnp.clip(noise * ramp, -12.0, 12.0)


def level_of(own_key, dims, split, smallest, high):
    level = 1.0
    for position, shards_of in split:
        steps = jax.random.uniform(jax.random.fold_in(jax.random.fold_in(own_key, 6), position), (shards_of,), jnp.float32, smallest / len(split), high / len(split))
        level = level * jnp.repeat(jnp.exp(steps), dims[position] // shards_of).reshape((-1,) + (1,) * (len(dims) - 1 - position))
    return level


def setup_inputs(seed: int = 0) -> dict:
    key_of = jax.random.split(jax.random.key(seed), 5)
    load_terms = draw_load_terms(jax.random.fold_in(key_of[4], 71), 0)
    geometry = jnp.clip(jnp.exp(math.log(0.2) - 2.3025851 * jax.random.uniform(key_of[1], (3, POINTS, POINTS, POINTS, NELEM), jnp.float32) ** level_of(key_of[1], (3, POINTS, POINTS, POINTS, NELEM), ((4, 32),), -0.2, 0.2)), 0.02, 0.2)
    mass_terms = jnp.clip(jnp.exp(math.log(4.0) - 1.3862944 * jax.random.uniform(key_of[2], (POINTS, POINTS, POINTS, NELEM), jnp.float32) ** level_of(key_of[2], (POINTS, POINTS, POINTS, NELEM), ((3, 32),), -0.2, 0.2)), 1.0, 4.0)
    element_order = jax.vmap(lambda own: jax.random.permutation(own, ELEM_DEV))(jax.random.split(key_of[3], N_SLAB)).reshape((N_SLAB, ELEM_DEV)).astype(jnp.int32)
    return dict(load_terms=load_terms, geometry=geometry, mass_terms=mass_terms, element_order=element_order)


spectrum_centre = 1.65
spectrum_half = 1.35


def legendre_table(positions, points):
    columns = [positions * 0.0 + 1.0, positions]
    for degree_now in range(2, points):
        columns.append(((2 * degree_now - 1) * positions * columns[-1] - (degree_now - 1) * columns[-2]) / degree_now)
    return np.stack(columns, axis=1)


def gll_derivative(points):
    degree = points - 1
    grid_nodes = -np.cos(np.pi * np.arange(points) / degree)
    for repeat in range(100):
        legendre = legendre_table(grid_nodes, points)
        grid_nodes = grid_nodes - (grid_nodes * legendre[:, degree] - legendre[:, degree - 1]) / (points * legendre[:, degree])
    legendre = legendre_table(grid_nodes, points)
    top_values = legendre[:, degree]
    index_list = np.arange(points)
    same_index = index_list[:, None] == index_list[None, :]
    spacing = grid_nodes[:, None] - grid_nodes[None, :]
    spacing = np.where(same_index, 1.0, spacing)
    deriv_table = top_values[:, None] / (top_values[None, :] * spacing)
    deriv_table = np.where(same_index, 0.0, deriv_table)
    deriv_table[0, 0] = -degree * points / 4.0
    deriv_table[degree, degree] = degree * points / 4.0
    return deriv_table


def local_apply(values, geometry, mass_terms, deriv_table):
    highest = lax.Precision.HIGHEST
    grad_one = jnp.einsum("ma,abce->mbce", deriv_table, values, precision=highest)
    result = jnp.einsum("ma,mbce->abce", deriv_table, geometry[0] * grad_one, precision=highest)
    grad_two = jnp.einsum("mb,abce->amce", deriv_table, values, precision=highest)
    result = result + jnp.einsum("mb,amce->abce", deriv_table, geometry[1] * grad_two, precision=highest)
    grad_three = jnp.einsum("mc,abce->abme", deriv_table, values, precision=highest)
    result = result + jnp.einsum("mc,abme->abce", deriv_table, geometry[2] * grad_three, precision=highest)
    return result + mass_terms * values


def local_diagonal(geometry, mass_terms, deriv_table):
    highest = lax.Precision.HIGHEST
    squared = deriv_table * deriv_table
    result = jnp.einsum("ma,mbce->abce", squared, geometry[0], precision=highest)
    result = result + jnp.einsum("mb,amce->abce", squared, geometry[1], precision=highest)
    result = result + jnp.einsum("mc,abme->abce", squared, geometry[2], precision=highest)
    return result + mass_terms


def to_grid(values, element_order):
    points = values.shape[0]
    inverse = jnp.argsort(element_order, axis=1).astype(jnp.int32)
    row_base = jnp.arange(N_SLAB, dtype=jnp.int32)[:, None] * ELEM_DEV
    picks = (row_base + inverse).reshape(-1).astype(jnp.int32)
    grid = jnp.take(values, picks, axis=3)
    return grid.reshape(points, points, points, N_SLAB * EL_X, EL_Y, EL_Z)


def to_store(grid, element_order):
    points = grid.shape[0]
    row_base = jnp.arange(N_SLAB, dtype=jnp.int32)[:, None] * ELEM_DEV
    picks = (row_base + element_order.astype(jnp.int32)).reshape(-1).astype(jnp.int32)
    return jnp.take(grid.reshape(points, points, points, NELEM), picks, axis=3)


def assemble_grid(grid):
    low_face = grid[0]
    high_face = grid[-1]
    shared = high_face + jnp.roll(low_face, -1, axis=2)
    grid = jnp.concatenate([jnp.roll(shared, 1, axis=2)[None], grid[1:-1], shared[None]], axis=0)
    low_face = grid[:, 0]
    high_face = grid[:, -1]
    zero_column = jnp.zeros_like(low_face[:, :, :, :1])
    new_high = high_face + jnp.concatenate([low_face[:, :, :, 1:], zero_column], axis=3)
    new_low = low_face + jnp.concatenate([zero_column, high_face[:, :, :, :-1]], axis=3)
    grid = jnp.concatenate([new_low[:, None], grid[:, 1:-1], new_high[:, None]], axis=1)
    low_face = grid[:, :, 0]
    high_face = grid[:, :, -1]
    shared = high_face + jnp.roll(low_face, -1, axis=4)
    grid = jnp.concatenate([jnp.roll(shared, 1, axis=4)[:, :, None], grid[:, :, 1:-1], shared[:, :, None]], axis=2)
    return grid


def grid_weights(points):
    node_ids = jnp.arange(points)
    end_node = (node_ids == 0) | (node_ids == points - 1)
    edge_mult = jnp.where(end_node, 2.0, 1.0).astype(jnp.float32)
    cross_ids = jnp.arange(EL_Y)
    low_shared = (node_ids == 0)[:, None] & (cross_ids > 0)[None, :]
    high_shared = (node_ids == points - 1)[:, None] & (cross_ids < EL_Y - 1)[None, :]
    mid_mult = jnp.where(low_shared | high_shared, 2.0, 1.0).astype(jnp.float32)
    total = edge_mult[:, None, None, None, None, None] * mid_mult[None, :, None, None, :, None] * edge_mult[None, None, :, None, None, None]
    full = jnp.broadcast_to(total, (points, points, points, N_SLAB * EL_X, EL_Y, EL_Z))
    return 1.0 / full


def reference(load_terms, geometry, mass_terms, element_order):
    points = load_terms.shape[0]
    deriv_table = jnp.asarray(gll_derivative(points), jnp.float32)

    def stiffness_sum(values):
        return to_store(assemble_grid(to_grid(values, element_order)), element_order)

    def operate(values):
        return stiffness_sum(local_apply(values, geometry, mass_terms, deriv_table))

    weight = to_store(grid_weights(points), element_order)
    start = stiffness_sum(load_terms)
    inv_diag = 1.0 / stiffness_sum(local_diagonal(geometry, mass_terms, deriv_table))
    ratio_sigma = spectrum_centre / spectrum_half
    step_vec = inv_diag * start / spectrum_centre
    precond = step_vec
    rho_prev = 1.0 / ratio_sigma
    for section in range(SECTIONS - 1):
        rho_next = 1.0 / (2.0 * ratio_sigma - rho_prev)
        misfit = start - operate(precond)
        step_vec = rho_next * rho_prev * step_vec + (2.0 * rho_next / spectrum_half) * inv_diag * misfit
        precond = precond + step_vec
        rho_prev = rho_next
    numerator = jnp.sum(weight * start * precond)
    image_vec = operate(precond)
    denominator = jnp.sum(weight * precond * image_vec)
    step_size = numerator / denominator
    return step_size * precond, start - step_size * image_vec
```

```python
import functools

import jax
import jax.numpy as jnp
import numpy as np
from jax import lax
from jax.experimental import pallas as pl
from jax.experimental.pallas import tpu as pltpu
from jax.sharding import PartitionSpec as P

EL_Y = 8
EL_Z = 16
MESH = pl.DeviceIdType.MESH
WIDEST = 32

spectrum_centre = 1.65
spectrum_half = 1.35


def legendre_table(positions, points):
    columns = [positions * 0.0 + 1.0, positions]
    for degree_now in range(2, points):
        columns.append(
            ((2 * degree_now - 1) * positions * columns[-1] - (degree_now - 1) * columns[-2])
            / degree_now
        )
    return np.stack(columns, axis=1)


def gll_derivative(points):
    degree = points - 1
    grid_nodes = -np.cos(np.pi * np.arange(points) / degree)
    for repeat in range(100):
        legendre = legendre_table(grid_nodes, points)
        grid_nodes = grid_nodes - (grid_nodes * legendre[:, degree] - legendre[:, degree - 1]) / (
            points * legendre[:, degree]
        )
    legendre = legendre_table(grid_nodes, points)
    top_values = legendre[:, degree]
    index_list = np.arange(points)
    same_index = index_list[:, None] == index_list[None, :]
    spacing = grid_nodes[:, None] - grid_nodes[None, :]
    spacing = np.where(same_index, 1.0, spacing)
    deriv_table = top_values[:, None] / (top_values[None, :] * spacing)
    deriv_table = np.where(same_index, 0.0, deriv_table)
    deriv_table[0, 0] = -degree * points / 4.0
    deriv_table[degree, degree] = degree * points / 4.0
    return deriv_table


def radices(count):
    factors = []
    while count > 1:
        width = max([w for w in range(2, WIDEST + 1) if count % w == 0], default=count)
        factors.append(width)
        count //= width
    return factors


def contract(values, table, symmetric):
    points = len(values)
    half = points // 2
    even = [values[j] + values[points - 1 - j] for j in range(half)]
    odd = [values[j] - values[points - 1 - j] for j in range(half)]
    low, high = [], []
    for m in range(half):
        a = [float(0.5 * (table[m, j] + table[m, points - 1 - j])) for j in range(half)]
        b = [float(0.5 * (table[m, j] - table[m, points - 1 - j])) for j in range(half)]
        part_even = a[0] * even[0]
        part_odd = b[0] * odd[0]
        for j in range(1, half):
            part_even = part_even + a[j] * even[j]
            part_odd = part_odd + b[j] * odd[j]
        low.append(part_even + part_odd)
        high.append(part_even - part_odd if symmetric else part_odd - part_even)
    return low + high[::-1]


def lane_gather(values, columns):
    dims = lax.GatherDimensionNumbers(
        offset_dims=(),
        collapsed_slice_dims=(1,),
        start_index_map=(1,),
        operand_batching_dims=(0,),
        start_indices_batching_dims=(0,),
    )
    return lax.gather(
        values, columns[..., None], dims, (1, 1), mode=lax.GatherScatterMode.PROMISE_IN_BOUNDS
    )


def kernel(
    count, points, factors, deriv,
    load_hbm, geo_hbm, mass_hbm, order_ref, sol_ref, res_ref,
    load, geo, mass, start, inverse, vec, work, image,
    face_out, face_in, own_inv, near_inv, coef, sums, *rest,
):
    parts_in = rest[: len(factors)]
    (in_sem, face_send, face_recv, inv_send, inv_recv, sum_send, sum_recv) = rest[len(factors):]
    me = lax.axis_index("slab")
    right = lax.rem(me + 1, count)
    left = lax.rem(me + count - 1, count)
    plane = points * points
    rows = points * plane
    last = rows - plane
    cols = load.shape[1]

    fetch = [
        pltpu.make_async_copy(geo_hbm, geo, in_sem.at[0]),
        pltpu.make_async_copy(mass_hbm, mass, in_sem.at[1]),
        pltpu.make_async_copy(load_hbm, load, in_sem.at[2]),
    ]
    for copy in fetch:
        copy.start()

    def peer(stride, width, k):
        digit = lax.rem(me // stride, width)
        return me + (lax.rem(digit + k, width) - digit) * stride

    strides = [int(np.prod(factors[:i])) for i in range(len(factors))]
    barrier = pltpu.get_barrier_semaphore()
    for near in (left, right):
        pl.semaphore_signal(barrier, inc=1, device_id=(near,), device_id_type=MESH)
    for stride, width in zip(strides, factors):
        @pl.loop(1, width)
        def _(k):
            pl.semaphore_signal(
                barrier, inc=1, device_id=(peer(stride, width, k),), device_id_type=MESH
            )

    cell = order_ref[...]
    cell8 = jnp.broadcast_to(cell, (points, cols))
    cell_col = jnp.transpose(jnp.broadcast_to(cell.astype(jnp.float32), (cols, cols)))
    lane = lax.broadcasted_iota(jnp.int32, (cols, cols), 1).astype(jnp.float32)
    source = lax.broadcasted_iota(jnp.int32, (cols, cols), 0).astype(jnp.float32)
    inv_row = jnp.sum(jnp.where(cell_col == lane, source, 0.0), axis=0, keepdims=True)
    inv8 = jnp.broadcast_to(inv_row.astype(jnp.int32), (points, cols))
    own_inv[...] = inv8
    pos_z = cell8 % EL_Z
    has_up = cell8 < cols - EL_Z
    has_down = cell8 >= EL_Z
    plus_y = lane_gather(inv8, jnp.where(has_up, cell8 + EL_Z, cell8))
    minus_y = lane_gather(inv8, jnp.where(has_down, cell8 - EL_Z, cell8))
    plus_z = lane_gather(inv8, jnp.where(pos_z == EL_Z - 1, cell8 - (EL_Z - 1), cell8 + 1))
    minus_z = lane_gather(inv8, jnp.where(pos_z == 0, cell8 + (EL_Z - 1), cell8 - 1))

    row_id = lax.broadcasted_iota(jnp.int32, (points, cols), 0)
    for t, table in enumerate((deriv, deriv.T, (deriv * deriv).T)):
        for k in range(points):
            vector = jnp.zeros((points, cols), jnp.float32)
            for m in range(points):
                vector = jnp.where(row_id == m, float(table[m, (m - k) % points]), vector)
            coef[t, k] = vector

    def rotate_contract(value, t):
        total = coef[t, 0] * value
        for k in range(1, points):
            total = total + coef[t, k] * pltpu.roll(value, k, 0)
        return total

    pl.semaphore_wait(barrier, 2 + sum(w - 1 for w in factors))

    def send_pair(low_src, high_src, low_dst, high_dst, send_sems, recv_sems):
        pair = [
            pltpu.make_async_remote_copy(
                src_ref=low_src, dst_ref=high_dst, send_sem=send_sems.at[0],
                recv_sem=recv_sems.at[1], device_id=(left,), device_id_type=MESH,
            ),
            pltpu.make_async_remote_copy(
                src_ref=high_src, dst_ref=low_dst, send_sem=send_sems.at[1],
                recv_sem=recv_sems.at[0], device_id=(right,), device_id_type=MESH,
            ),
        ]
        for copy in pair:
            copy.start()
        return pair

    def send_faces(e):
        return send_pair(
            face_out.at[e, 0], face_out.at[e, 1], face_in.at[e, 0], face_in.at[e, 1],
            face_send.at[e], face_recv.at[e],
        )

    pair_load = send_pair(
        load_hbm.at[pl.ds(0, plane)], load_hbm.at[pl.ds(last, plane)],
        face_in.at[0, 0], face_in.at[0, 1], face_send.at[0], face_recv.at[0],
    )
    pair_inv = send_pair(own_inv, own_inv, near_inv.at[0], near_inv.at[1], inv_send, inv_recv)

    def at(base, b):
        return pl.ds(pl.multiple_of(base + b * points, points), points)

    def geo_at(k, base, b):
        return pl.ds(pl.multiple_of(k * rows + base + b * points, points), points)

    def store_face(e, side, b, value):
        face_out[e, side, pl.ds(b * points, points)] = value

    def assemble_plane(ref, base):
        low = ref[at(base, 0)]
        high = ref[at(base, points - 1)]
        ref[at(base, points - 1)] = high + jnp.where(has_up, lane_gather(low, plus_y), 0.0)
        ref[at(base, 0)] = low + jnp.where(has_down, lane_gather(high, minus_y), 0.0)
        first = pl.ds(base, points, stride=points)
        end = pl.ds(base + points - 1, points, stride=points)
        low = ref[first]
        high = ref[end]
        ref[end] = high + lane_gather(low, plus_z)
        ref[first] = low + lane_gather(high, minus_z)

    square = deriv * deriv
    fetch[0].wait()
    fetch[1].wait()

    @pl.loop(0, points)
    def _(b):
        values = [geo[geo_at(0, a * plane, b)] for a in range(points)]
        for a, value in enumerate(contract(values, square.T, True)):
            work[at(a * plane, b)] = value

    def diagonal_plane(base, put):
        values = [geo[geo_at(1, base, b)] for b in range(points)]
        for b, value in enumerate(contract(values, square.T, True)):
            value = value + rotate_contract(geo[geo_at(2, base, b)], 2)
            put(b, value + work[at(base, b)] + mass[at(base, b)])

    diagonal_plane(0, functools.partial(store_face, 1, 0))
    diagonal_plane(last, functools.partial(store_face, 1, 1))
    pair_diag = send_faces(1)

    def first_update(base):
        for b in range(points):
            span = at(base, b)
            scaled = 1.0 / inverse[span]
            inverse[span] = scaled
            vec[span] = scaled * start[span] * (1.0 / spectrum_centre)

    fetch[2].wait()

    @pl.loop(1, points - 1)
    def _(a):
        base = pl.multiple_of(a * plane, plane)

        def put(b, value):
            inverse[at(base, b)] = value

        diagonal_plane(base, put)
        for b in range(points):
            start[at(base, b)] = load[at(base, b)]
        assemble_plane(start, base)
        assemble_plane(inverse, base)
        first_update(base)

    for copy in pair_inv:
        copy.wait()
    minus_x = lane_gather(near_inv[0], cell8)
    plus_x = lane_gather(near_inv[1], cell8)

    def join_face(e, side, own, ref):
        base = (0, last)[side]
        columns = (minus_x, plus_x)[side]
        for b in range(points):
            ref[at(base, b)] = own(b) + lane_gather(
                face_in[e, side, pl.ds(b * points, points)], columns
            )
        assemble_plane(ref, base)

    def own_face(e, side):
        return lambda b: face_out[e, side, pl.ds(b * points, points)]

    for copy in pair_load:
        copy.wait()
    for side in (0, 1):
        base = (0, last)[side]
        join_face(0, side, lambda b: load[at(base, b)], start)
    for copy in pair_diag:
        copy.wait()
    for side in (0, 1):
        join_face(1, side, own_face(1, side), inverse)
        first_update((0, last)[side])

    def gradient_first():
        @pl.loop(0, points)
        def _(b):
            values = [vec[at(a * plane, b)] for a in range(points)]
            slopes = contract(values, deriv, False)
            fluxes = [geo[geo_at(0, a * plane, b)] * slopes[a] for a in range(points)]
            for a, value in enumerate(contract(fluxes, deriv.T, False)):
                work[at(a * plane, b)] = value

    def operate_plane(base, put):
        values = [vec[at(base, b)] for b in range(points)]
        slopes = contract(values, deriv, False)
        fluxes = [geo[geo_at(1, base, b)] * slopes[b] for b in range(points)]
        for b, value in enumerate(contract(fluxes, deriv.T, False)):
            flux = geo[geo_at(2, base, b)] * rotate_contract(values[b], 0)
            value = value + rotate_contract(flux, 1)
            put(b, values[b], value + work[at(base, b)] + mass[at(base, b)] * values[b])

    ratio_sigma = spectrum_centre / spectrum_half
    rho_prev = 1.0 / ratio_sigma
    rho_next = 1.0 / (2.0 * ratio_sigma - rho_prev)
    on_misfit = 2.0 * rho_next / spectrum_half
    on_start = (1.0 + rho_next * rho_prev) / spectrum_centre + on_misfit

    def second_update(base):
        for b in range(points):
            span = at(base, b)
            vec[span] = inverse[span] * (on_start * start[span] - on_misfit * image[span])

    gradient_first()
    for side in (0, 1):
        operate_plane((0, last)[side], lambda b, v, out: store_face(2, side, b, out))
    pair_first = send_faces(2)

    @pl.loop(1, points - 1)
    def _(a):
        base = pl.multiple_of(a * plane, plane)

        def put(b, value, out):
            image[at(base, b)] = out

        operate_plane(base, put)
        assemble_plane(image, base)
        second_update(base)

    for copy in pair_first:
        copy.wait()
    for side in (0, 1):
        join_face(2, side, own_face(2, side), image)
        second_update((0, last)[side])

    gradient_first()
    tally = [jnp.zeros((points, cols), jnp.float32)] * 2

    def add_up(tally, base, b, value, out):
        return [tally[0] + load[at(base, b)] * value, tally[1] + value * out]

    for side in (0, 1):
        base = (0, last)[side]

        def put(b, value, out):
            nonlocal tally
            store_face(3, side, b, out)
            tally = add_up(tally, base, b, value, out)

        operate_plane(base, put)
    pair_second = send_faces(3)

    def plane_step(a, carry):
        base = pl.multiple_of(a * plane, plane)
        state = list(carry)

        def put(b, value, out):
            nonlocal state
            image[at(base, b)] = out
            state = add_up(state, base, b, value, out)

        operate_plane(base, put)
        return tuple(state)

    tally = lax.fori_loop(1, points - 1, plane_step, tuple(tally))
    total = jnp.concatenate([jnp.sum(part, axis=0, keepdims=True) for part in tally], axis=1)

    def sum_copy(i, k):
        stride, width = strides[i], factors[i]
        return pltpu.make_async_remote_copy(
            src_ref=sums.at[i], dst_ref=parts_in[i].at[k - 1],
            send_sem=sum_send.at[i, k - 1], recv_sem=sum_recv.at[i, k - 1],
            device_id=(peer(stride, width, k),), device_id_type=MESH,
        )

    def start_sum(i, value):
        sums[i] = value

        @pl.loop(1, factors[i])
        def _(k):
            sum_copy(i, k).start()

    def finish_sum(i, value):
        @pl.loop(1, factors[i])
        def _(k):
            sum_copy(i, k).wait()

        for k in range(factors[i] - 1):
            value = value + parts_in[i][k]
        return value

    start_sum(0, total)

    @pl.loop(1, points - 1)
    def _(a):
        assemble_plane(image, pl.multiple_of(a * plane, plane))

    for copy in pair_second:
        copy.wait()
    for side in (0, 1):
        join_face(3, side, own_face(3, side), image)
    for i in range(len(factors)):
        if i:
            start_sum(i, total)
        total = finish_sum(i, total)
    numerator = jnp.sum(total[:, :cols], axis=1, keepdims=True)
    denominator = jnp.sum(total[:, cols:], axis=1, keepdims=True)
    size = jnp.broadcast_to(numerator / denominator, (points, cols))

    @pl.loop(0, points)
    def _(a):
        base = pl.multiple_of(a * plane, plane)
        for b in range(points):
            span = at(base, b)
            sol_ref[span] = size * vec[span]
            res_ref[span] = start[span] - size * image[span]


def on_device(count, load_terms, geometry, mass_terms, element_order):
    points = load_terms.shape[0]
    cols = load_terms.shape[3]
    plane = points * points
    rows = points * plane
    deriv = gll_derivative(points)
    factors = radices(count)
    field = jax.ShapeDtypeStruct((rows, cols), jnp.float32)
    f32 = jnp.float32
    big = [pltpu.VMEM((rows, cols), f32)]
    scratch = (
        big + [pltpu.VMEM((3 * rows, cols), f32)] + big * 6
        + [
            pltpu.VMEM((4, 2, plane, cols), f32),
            pltpu.VMEM((4, 2, plane, cols), f32),
            pltpu.VMEM((points, cols), jnp.int32),
            pltpu.VMEM((2, points, cols), jnp.int32),
            pltpu.VMEM((3, points, points, cols), f32),
            pltpu.VMEM((len(factors), 1, 2 * cols), f32),
        ]
        + [pltpu.VMEM((w - 1, 1, 2 * cols), f32) for w in factors]
        + [
            pltpu.SemaphoreType.DMA((3,)),
            pltpu.SemaphoreType.DMA((4, 2)),
            pltpu.SemaphoreType.DMA((4, 2)),
            pltpu.SemaphoreType.DMA((2,)),
            pltpu.SemaphoreType.DMA((2,)),
            pltpu.SemaphoreType.DMA((len(factors), max(factors) - 1)),
            pltpu.SemaphoreType.DMA((len(factors), max(factors) - 1)),
        ]
    )
    hbm = pl.BlockSpec(memory_space=pl.ANY)
    vmem = pl.BlockSpec(memory_space=pltpu.VMEM)
    solution_rows, residual_rows = pl.pallas_call(
        functools.partial(kernel, count, points, factors, deriv),
        out_shape=(field, field),
        in_specs=[hbm, hbm, hbm, vmem],
        out_specs=(vmem, vmem),
        scratch_shapes=scratch,
        compiler_params=pltpu.CompilerParams(collective_id=0, has_side_effects=True),
    )(
        load_terms.reshape(rows, cols),
        geometry.reshape(3 * rows, cols),
        mass_terms.reshape(rows, cols),
        element_order,
    )
    shape = load_terms.shape
    return solution_rows.reshape(shape), residual_rows.reshape(shape)


def solution(mesh):
    placed = (
        P(None, None, None, "slab"),
        P(None, None, None, None, "slab"),
        P(None, None, None, "slab"),
        P("slab", None),
    )
    return jax.shard_map(
        functools.partial(on_device, mesh.shape["slab"]),
        mesh=mesh,
        in_specs=placed,
        out_specs=(P(None, None, None, "slab"), P(None, None, None, "slab")),
        check_vma=False,
    )
```

```python
import functools

import jax
import jax.numpy as jnp
import numpy as np
from jax import lax
from jax.experimental import pallas as pl
from jax.experimental.pallas import tpu as pltpu
from jax.sharding import PartitionSpec as P

EL_Y = 8
EL_Z = 16
MESH = pl.DeviceIdType.MESH
WIDEST = 32

spectrum_centre = 1.65
spectrum_half = 1.35


def legendre_table(positions, points):
    columns = [positions * 0.0 + 1.0, positions]
    for degree_now in range(2, points):
        columns.append(
            ((2 * degree_now - 1) * positions * columns[-1] - (degree_now - 1) * columns[-2])
            / degree_now
        )
    return np.stack(columns, axis=1)


def gll_derivative(points):
    degree = points - 1
    grid_nodes = -np.cos(np.pi * np.arange(points) / degree)
    for repeat in range(100):
        legendre = legendre_table(grid_nodes, points)
        grid_nodes = grid_nodes - (grid_nodes * legendre[:, degree] - legendre[:, degree - 1]) / (
            points * legendre[:, degree]
        )
    legendre = legendre_table(grid_nodes, points)
    top_values = legendre[:, degree]
    index_list = np.arange(points)
    same_index = index_list[:, None] == index_list[None, :]
    spacing = grid_nodes[:, None] - grid_nodes[None, :]
    spacing = np.where(same_index, 1.0, spacing)
    deriv_table = top_values[:, None] / (top_values[None, :] * spacing)
    deriv_table = np.where(same_index, 0.0, deriv_table)
    deriv_table[0, 0] = -degree * points / 4.0
    deriv_table[degree, degree] = degree * points / 4.0
    return deriv_table


def radices(count):
    factors = []
    while count > 1:
        width = max([w for w in range(2, WIDEST + 1) if count % w == 0], default=count)
        factors.append(width)
        count //= width
    return factors


def contract(values, table, symmetric):
    points = len(values)
    half = points // 2
    even = [values[j] + values[points - 1 - j] for j in range(half)]
    odd = [values[j] - values[points - 1 - j] for j in range(half)]
    low, high = [], []
    for m in range(half):
        a = [float(0.5 * (table[m, j] + table[m, points - 1 - j])) for j in range(half)]
        b = [float(0.5 * (table[m, j] - table[m, points - 1 - j])) for j in range(half)]
        part_even = a[0] * even[0]
        part_odd = b[0] * odd[0]
        for j in range(1, half):
            part_even = part_even + a[j] * even[j]
            part_odd = part_odd + b[j] * odd[j]
        low.append(part_even + part_odd)
        high.append(part_even - part_odd if symmetric else part_odd - part_even)
    return low + high[::-1]


def lane_gather(values, columns):
    dims = lax.GatherDimensionNumbers(
        offset_dims=(),
        collapsed_slice_dims=(1,),
        start_index_map=(1,),
        operand_batching_dims=(0,),
        start_indices_batching_dims=(0,),
    )
    return lax.gather(
        values, columns[..., None], dims, (1, 1), mode=lax.GatherScatterMode.PROMISE_IN_BOUNDS
    )


def kernel(
    count, points, factors, deriv,
    load_hbm, geo_hbm, mass_hbm, order_hbm, sol_ref, res_ref,
    load, geo, mass, start, inverse, vec, work, image,
    face_out, face_in, own_inv, near_inv, order, coef, sums, *rest,
):
    parts_in = rest[: len(factors)]
    (in_sem, face_send, face_recv, inv_sem, sum_send, sum_recv) = rest[len(factors):]
    me = lax.axis_index("slab")
    right = lax.rem(me + 1, count)
    left = lax.rem(me + count - 1, count)
    plane = points * points
    rows = points * plane
    last = rows - plane
    cols = load.shape[1]

    fetch = [
        pltpu.make_async_copy(geo_hbm, geo, in_sem.at[0]),
        pltpu.make_async_copy(mass_hbm, mass, in_sem.at[1]),
        pltpu.make_async_copy(load_hbm, load, in_sem.at[2]),
        pltpu.make_async_copy(order_hbm, order, in_sem.at[3]),
    ]
    for copy in fetch[::-1][:1] + fetch[:3]:
        copy.start()

    def peer(stride, width, k):
        digit = lax.rem(me // stride, width)
        return me + (lax.rem(digit + k, width) - digit) * stride

    strides = [int(np.prod(factors[:i])) for i in range(len(factors))]
    barrier = pltpu.get_barrier_semaphore()
    for near in (left, right):
        pl.semaphore_signal(barrier, inc=1, device_id=(near,), device_id_type=MESH)
    for stride, width in zip(strides, factors):
        @pl.loop(1, width)
        def _(k):
            pl.semaphore_signal(
                barrier, inc=1, device_id=(peer(stride, width, k),), device_id_type=MESH
            )

    fetch[3].wait()
    cell = order[...]
    cell8 = jnp.broadcast_to(cell, (points, cols))
    cell_col = jnp.transpose(jnp.broadcast_to(cell.astype(jnp.float32), (cols, cols)))
    lane = lax.broadcasted_iota(jnp.int32, (cols, cols), 1).astype(jnp.float32)
    source = lax.broadcasted_iota(jnp.int32, (cols, cols), 0).astype(jnp.float32)
    inv_row = jnp.sum(jnp.where(cell_col == lane, source, 0.0), axis=0, keepdims=True)
    inv8 = jnp.broadcast_to(inv_row.astype(jnp.int32), (points, cols))
    own_inv[...] = inv8
    pos_z = cell8 % EL_Z
    has_up = cell8 < cols - EL_Z
    has_down = cell8 >= EL_Z
    plus_y = lane_gather(inv8, jnp.where(has_up, cell8 + EL_Z, cell8))
    minus_y = lane_gather(inv8, jnp.where(has_down, cell8 - EL_Z, cell8))
    plus_z = lane_gather(inv8, jnp.where(pos_z == EL_Z - 1, cell8 - (EL_Z - 1), cell8 + 1))
    minus_z = lane_gather(inv8, jnp.where(pos_z == 0, cell8 + (EL_Z - 1), cell8 - 1))

    row_id = lax.broadcasted_iota(jnp.int32, (points, cols), 0)
    for t, table in enumerate((deriv, deriv.T, (deriv * deriv).T)):
        for k in range(points):
            vector = jnp.zeros((points, cols), jnp.float32)
            for m in range(points):
                vector = jnp.where(row_id == m, float(table[m, (m - k) % points]), vector)
            coef[t, k] = vector

    def rotate_contract(value, t):
        total = coef[t, 0] * value
        for k in range(1, points):
            total = total + coef[t, k] * pltpu.roll(value, k, 0)
        return total

    def send_pair(low_src, high_src, dst, send_sem, recv_sem):
        for src, side, near in ((low_src, 1, left), (high_src, 0, right)):
            pltpu.make_async_remote_copy(
                src_ref=src, dst_ref=dst.at[side], send_sem=send_sem, recv_sem=recv_sem,
                device_id=(near,), device_id_type=MESH,
            ).start()

    def settle(ref, send_sem, recv_sem):
        return pltpu.make_async_remote_copy(
            src_ref=ref, dst_ref=ref, send_sem=send_sem, recv_sem=recv_sem,
            device_id=(right,), device_id_type=MESH,
        )

    def send_faces(e):
        send_pair(face_out.at[e, 0], face_out.at[e, 1], face_in.at[e], face_send, face_recv.at[e])

    def wait_faces(e):
        settle(face_in.at[e], face_send, face_recv.at[e]).wait_recv()

    def at(base, b):
        return pl.ds(base + b * points, points)

    def geo_at(k, base, b):
        return pl.ds(k * rows + base + b * points, points)

    def store_face(e, side, b, value):
        face_out[e, side, pl.ds(b * points, points)] = value

    inner = [a * plane for a in range(1, points - 1)]

    def assemble_planes(spots):
        lows = [ref[at(base, 0)] for ref, base in spots]
        highs = [ref[at(base, points - 1)] for ref, base in spots]
        from_low = [lane_gather(low, plus_y) for low in lows]
        from_high = [lane_gather(high, minus_y) for high in highs]
        for i, (ref, base) in enumerate(spots):
            ref[at(base, points - 1)] = highs[i] + jnp.where(has_up, from_low[i], 0.0)
            ref[at(base, 0)] = lows[i] + jnp.where(has_down, from_high[i], 0.0)
        firsts = [pl.ds(base, points, stride=points) for _, base in spots]
        ends = [pl.ds(base + points - 1, points, stride=points) for _, base in spots]
        lows = [ref[first] for (ref, _), first in zip(spots, firsts)]
        highs = [ref[end] for (ref, _), end in zip(spots, ends)]
        from_low = [lane_gather(low, plus_z) for low in lows]
        from_high = [lane_gather(high, minus_z) for high in highs]
        for i, (ref, _) in enumerate(spots):
            ref[ends[i]] = highs[i] + from_low[i]
            ref[firsts[i]] = lows[i] + from_high[i]

    square = deriv * deriv
    fetch[0].wait()
    fetch[1].wait()

    for b in range(points):
        values = [geo[geo_at(0, a * plane, b)] for a in range(points)]
        for a, value in enumerate(contract(values, square.T, True)):
            work[at(a * plane, b)] = value

    def diagonal_plane(base, put):
        values = [geo[geo_at(1, base, b)] for b in range(points)]
        for b, value in enumerate(contract(values, square.T, True)):
            value = value + rotate_contract(geo[geo_at(2, base, b)], 2)
            put(b, value + work[at(base, b)] + mass[at(base, b)])

    diagonal_plane(0, functools.partial(store_face, 1, 0))
    diagonal_plane(last, functools.partial(store_face, 1, 1))
    pl.semaphore_wait(barrier, 2 + sum(w - 1 for w in factors))
    send_pair(
        load_hbm.at[pl.ds(0, plane)], load_hbm.at[pl.ds(last, plane)],
        face_in.at[0], face_send, face_recv.at[0],
    )
    send_pair(own_inv, own_inv, near_inv, inv_sem.at[0], inv_sem.at[1])
    send_faces(1)

    def first_update(base):
        for b in range(points):
            span = at(base, b)
            scaled = 1.0 / inverse[span]
            inverse[span] = scaled
            vec[span] = scaled * start[span] * (1.0 / spectrum_centre)

    fetch[2].wait()

    for base in inner:
        for b in range(points):
            start[at(base, b)] = load[at(base, b)]
    assemble_planes([(start, base) for base in inner])
    for base in inner:

        def put(b, value):
            inverse[at(base, b)] = value

        diagonal_plane(base, put)
    assemble_planes([(inverse, base) for base in inner])
    for base in inner:
        first_update(base)

    def along_first(put):
        for b in range(points):
            values = [vec[at(a * plane, b)] for a in range(points)]
            slopes = contract(values, deriv, False)
            fluxes = [geo[geo_at(0, a * plane, b)] * slopes[a] for a in range(points)]
            for a, value in enumerate(contract(fluxes, deriv.T, False)):
                put(a, b, value)

    def in_plane(base, ref):
        values = [vec[at(base, b)] for b in range(points)]
        slopes = contract(values, deriv, False)
        fluxes = [geo[geo_at(1, base, b)] * slopes[b] for b in range(points)]
        for b, value in enumerate(contract(fluxes, deriv.T, False)):
            flux = geo[geo_at(2, base, b)] * rotate_contract(values[b], 0)
            value = value + rotate_contract(flux, 1)
            ref[at(base, b)] = value + mass[at(base, b)] * values[b]

    def apply_faces_first(e, extra):
        for base in (0, last):
            in_plane(base, work)

        def put(a, b, term):
            span = at(a * plane, b)
            if a in (0, points - 1):
                out = work[span] + term
                store_face(e, int(a > 0), b, out)
            else:
                out = image[span] + term
                image[span] = out
            extra(span, out)

        along_first(put)
        send_faces(e)

    for base in inner:
        in_plane(base, image)

    settle(near_inv, inv_sem.at[0], inv_sem.at[1]).wait()
    minus_x = lane_gather(near_inv[0], cell8)
    plus_x = lane_gather(near_inv[1], cell8)

    def join_faces(e, own, ref):
        for side, (base, columns) in enumerate(((0, minus_x), (last, plus_x))):
            for b in range(points):
                ref[at(base, b)] = own(side, b) + lane_gather(
                    face_in[e, side, pl.ds(b * points, points)], columns
                )
        assemble_planes([(ref, 0), (ref, last)])

    def own_face(e):
        return lambda side, b: face_out[e, side, pl.ds(b * points, points)]

    wait_faces(0)
    join_faces(0, lambda side, b: load[at((0, last)[side], b)], start)
    wait_faces(1)
    join_faces(1, own_face(1), inverse)
    first_update(0)
    first_update(last)

    ratio_sigma = spectrum_centre / spectrum_half
    rho_prev = 1.0 / ratio_sigma
    rho_next = 1.0 / (2.0 * ratio_sigma - rho_prev)
    on_misfit = 2.0 * rho_next / spectrum_half
    on_start = (1.0 + rho_next * rho_prev) / spectrum_centre + on_misfit

    def second_update(base):
        for b in range(points):
            span = at(base, b)
            vec[span] = inverse[span] * (on_start * start[span] - on_misfit * image[span])

    apply_faces_first(2, lambda span, out: None)
    assemble_planes([(image, base) for base in inner])
    for base in inner:
        second_update(base)

    def sum_of(terms):
        while len(terms) > 1:
            terms = [x + y for x, y in zip(terms[::2], terms[1::2])] + terms[len(terms) & ~1:]
        return terms[0]

    def load_product(base):
        return sum_of([load[at(base, b)] * vec[at(base, b)] for b in range(points)])

    for base in inner:
        in_plane(base, image)
    on_load = sum_of([load_product(base) for base in inner])

    wait_faces(2)
    join_faces(2, own_face(2), image)
    second_update(0)
    second_update(last)

    products = []
    apply_faces_first(3, lambda span, out: products.append(vec[span] * out))
    on_load = on_load + load_product(0) + load_product(last)
    tally = [on_load, sum_of(products)]
    total = jnp.concatenate([jnp.sum(part, axis=0, keepdims=True) for part in tally], axis=1)

    def sum_copy(i, k):
        stride, width = strides[i], factors[i]
        return pltpu.make_async_remote_copy(
            src_ref=sums.at[i], dst_ref=parts_in[i].at[k - 1],
            send_sem=sum_send.at[i], recv_sem=sum_recv.at[i],
            device_id=(peer(stride, width, k),), device_id_type=MESH,
        )

    def start_sum(i, value):
        sums[i] = value

        @pl.loop(1, factors[i])
        def _(k):
            sum_copy(i, k).start()

    def finish_sum(i, value):
        settle(parts_in[i], sum_send.at[i], sum_recv.at[i]).wait()
        for k in range(factors[i] - 1):
            value = value + parts_in[i][k]
        return value

    start_sum(0, total)

    assemble_planes([(image, base) for base in inner])

    wait_faces(3)
    join_faces(3, own_face(3), image)
    for i in range(len(factors)):
        if i:
            start_sum(i, total)
        total = finish_sum(i, total)
    settle(face_out, face_send, face_recv.at[0]).wait_send()
    numerator = jnp.sum(total[:, :cols], axis=1, keepdims=True)
    denominator = jnp.sum(total[:, cols:], axis=1, keepdims=True)
    size = jnp.broadcast_to(numerator / denominator, (points, cols))

    for a in range(points):
        for b in range(points):
            span = at(a * plane, b)
            sol_ref[span] = size * vec[span]
            res_ref[span] = start[span] - size * image[span]


def on_device(count, load_terms, geometry, mass_terms, element_order):
    points = load_terms.shape[0]
    cols = load_terms.shape[3]
    plane = points * points
    rows = points * plane
    deriv = gll_derivative(points)
    factors = radices(count)
    f32 = jnp.float32
    big = [pltpu.VMEM((rows, cols), f32)]
    scratch = (
        big + [pltpu.VMEM((3 * rows, cols), f32)] + big * 6
        + [
            pltpu.VMEM((4, 2, plane, cols), f32),
            pltpu.VMEM((4, 2, plane, cols), f32),
            pltpu.VMEM((points, cols), jnp.int32),
            pltpu.VMEM((2, points, cols), jnp.int32),
            pltpu.VMEM((1, cols), jnp.int32),
            pltpu.VMEM((3, points, points, cols), f32),
            pltpu.VMEM((len(factors), 1, 2 * cols), f32),
        ]
        + [pltpu.VMEM((w - 1, 1, 2 * cols), f32) for w in factors]
        + [
            pltpu.SemaphoreType.DMA((4,)),
            pltpu.SemaphoreType.DMA,
            pltpu.SemaphoreType.DMA((4,)),
            pltpu.SemaphoreType.DMA((2,)),
            pltpu.SemaphoreType.DMA((len(factors),)),
            pltpu.SemaphoreType.DMA((len(factors),)),
        ]
    )
    hbm = pl.BlockSpec(memory_space=pl.ANY)
    vmem = pl.BlockSpec(memory_space=pltpu.VMEM)
    solution_rows, residual_rows = pl.pallas_call(
        functools.partial(kernel, count, points, factors, deriv),
        out_shape=(pltpu.VMEM((rows, cols), f32),) * 2,
        in_specs=[hbm] * 4,
        out_specs=(vmem, vmem),
        scratch_shapes=scratch,
        compiler_params=pltpu.CompilerParams(collective_id=0, has_side_effects=True),
    )(
        load_terms.reshape(rows, cols),
        geometry.reshape(3 * rows, cols),
        mass_terms.reshape(rows, cols),
        element_order,
    )
    shape = load_terms.shape
    return solution_rows.reshape(shape), residual_rows.reshape(shape)


def solution(mesh):
    placed = (
        P(None, None, None, "slab"),
        P(None, None, None, None, "slab"),
        P(None, None, None, "slab"),
        P("slab", None),
    )
    return jax.shard_map(
        functools.partial(on_device, mesh.shape["slab"]),
        mesh=mesh,
        in_specs=placed,
        out_specs=(P(None, None, None, "slab"), P(None, None, None, "slab")),
        check_vma=False,
    )
```
